512 devices in a mesh: row: 64 (over x, y, z_hi), col: 8 (over z_lo, core).
Axes of the slice: x: 4, y: 8, z: 8 (z_hi: 2, z_lo: 4; z = z_hi * 4 + z_lo), core: 2. Of those that a mesh axis runs over, the one named last changes fastest.
Arguments:
- features: float32 [16384, 512], P('row', 'col'), may hold values from -20 to 20
- adj_values: bfloat16 [256, 64, 4096], P('row', 'col'), may hold values from 0 to 0.0078125
- adj_cols: int32 [256, 64], P('row', 'col'), may hold values from 0 to 255, as said below
- adj_count: int32 [256], P('row'), may hold values from 16 to 64, as said below
Outputs:
- hop_one: float32 [16384, 512], P('row', 'col')
- hop_two: float32 [16384, 512], P('row', 'col')
The draws below stay inside these ranges and needn't reach their ends.
Inputs may be any that keep to these rules, and one draw needn't show every extreme that they name: `adj_cols`: within one row block the column blocks of all 64 slots are distinct. `adj_count`: some row block has all 64 slots live.
All inputs are finite; a program needn't handle non-finite values.
Results may differ from the reference program's by a relative error of at most 0.0003.
Values may be sent and summed in bfloat16 or wider, within the bound.
A program may use at most 128 MiB of HBM per device.

```python
import jax
import jax.numpy as jnp
from jax import lax

F = 512
BLK = 64
K = 64
NB = 256
NODES = 16384


def draw_features(key, part):
    mean_key = jax.random.fold_in(key, 31)
    sign_key = jax.random.fold_in(key, 37)
    noise_key = jax.random.fold_in(key, 41)
    signs = jnp.where(jax.random.bernoulli(sign_key, 0.5, (F,)), 1.0, -1.0).astype(jnp.float32)
    column_mean = jax.random.uniform(mean_key, (F,), jnp.float32, 0.5, 1.5) * signs
    noise = jnp.clip(jax.random.normal(noise_key, (NODES, F), jnp.float32), -5.0, 5.0) * 3.0
    return (column_mean[None, :] + noise).astype(jnp.float32)


def draw_adj_values(key, part):
    value_key = jax.random.fold_in(key, 43)
    edge_key = jax.random.fold_in(key, 47)
    tile_shape = (NB, K, BLK * BLK)
    edge_mask = (jax.random.randint(edge_key, tile_shape, 0, 16) == 0).astype(jnp.float32)
    entry_values = jax.random.uniform(value_key, tile_shape, jnp.float32, 0.0, 32.0 / (BLK * K))
    return (entry_values * edge_mask).astype(jnp.bfloat16)


def draw_adj_cols(key, part):
    row_keys = jax.random.split(jax.random.fold_in(key, 17), NB)

    def one_row(row_key):
        return jax.random.permutation(row_key, NB)[:K].astype(jnp.int32)
    return jax.vmap(one_row)(row_keys)


def draw_adj_count(key, part):
    first_key = jax.random.fold_in(key, 23)
    second_key = jax.random.fold_in(key, 29)
    counts = jax.random.randint(first_key, (NB,), K // 4, K + 1).astype(jnp.int32)
    chosen = jax.random.randint(second_key, (), 0, NB)
    return counts.at[chosen].set(K)


def setup_inputs(seed: int = 0) -> dict:
    splits = jax.random.split(jax.random.key(seed), 5)
    return {
        "features": draw_features(jax.random.fold_in(splits[4], 71), 0),
        "adj_values": draw_adj_values(jax.random.fold_in(splits[4], 71), 0),
        "adj_cols": draw_adj_cols(jax.random.fold_in(splits[4], 71), 0),
        "adj_count": draw_adj_count(jax.random.fold_in(splits[4], 71), 0),
    }


def propagate(matrix, adj_values, adj_cols, adj_count):
    feat_width = matrix.shape[1]
    blocks = matrix.reshape(NB, BLK, feat_width)
    slot_ids = jnp.arange(K, dtype=jnp.int32)
    live_mask = (slot_ids[None, :] < adj_count[:, None]).astype(jnp.float32)

    def single(record):
        tile_set, col_ids, slot_mask = record
        picked = blocks[col_ids]
        weights = tile_set.astype(jnp.float32).reshape(K, BLK, BLK) * slot_mask[:, None, None]
        return jnp.einsum("kij,kjf->if", weights, picked, precision=lax.Precision.HIGHEST)

    result = lax.map(single, (adj_values, adj_cols, live_mask))
    return result.reshape(NB * BLK, feat_width)


def reference(features, adj_values, adj_cols, adj_count):
    hop_one = propagate(features, adj_values, adj_cols, adj_count)
    hop_two = propagate(hop_one, adj_values, adj_cols, adj_count)
    return (hop_one, hop_two)
```

```python
import functools

import jax
import jax.numpy as jnp
from jax import lax
from jax.experimental import pallas as pl
from jax.experimental.pallas import tpu as pltpu
from jax.sharding import PartitionSpec as P

BLK = 64
NX, NY, NZ = 4, 8, 2
NC = 8
MESH = pl.DeviceIdType.MESH


def split_parts(x):
    hi = x.astype(jnp.bfloat16)
    lo = (x - hi.astype(jnp.float32)).astype(jnp.bfloat16)
    return jnp.concatenate([hi, lo], axis=-1)


def pack_kernel(x_ref, out_ref):
    out_ref[...] = split_parts(x_ref[...])


def pack(features):
    return pl.pallas_call(
        pack_kernel,
        out_shape=jax.ShapeDtypeStruct((256, 2 * BLK), jnp.bfloat16),
    )(features)


def ring_program():
    def stream(rel, half):
        tag = (rel, half)
        first, second = ("x", "y") if half == 0 else ("y", "x")
        size = {"x": NX, "y": NY}

        def phase(axis, whole):
            n = size[axis]
            steps = []
            for t in range(1, n // 2 + 1):
                sends = []
                for sign in (1, -1):
                    off = -sign * (t - 1)
                    slab = (off, whole) if axis == "x" else (whole, off)
                    sub = None if t < n // 2 else (0 if sign == 1 else 1)
                    sends.append(((tag, axis, t, sign), rel, half, slab, sub, axis, sign))
                steps.append(sends)
            return steps

        return phase(first, 0) + phase(second, None)

    program = []
    for rel in (0, 1):
        for half in (0, 1):
            steps = stream(rel, half)
            for t, sends in enumerate(steps):
                needs = [] if t == 0 else [s[0] for s in steps[t - 1]]
                if t == 0 and rel == 1:
                    needs = ["z"]
                program.append((t + 2 * rel, rel, half, needs, sends))
            program.append((len(steps) + 2 * rel, rel, half, [s[0] for s in steps[-1]], []))
    program.sort(key=lambda p: p[0])
    return program


def gather_kernel(with_adj, *refs):
    if with_adj:
        shard, tiles, cols, nodes, tiles_all, cols_all, send, recv, local, adj_send, adj_recv, adj_local = refs
    else:
        shard, nodes, send, recv, local = refs
    row = lax.axis_index("row")
    col = lax.axis_index("col")
    zh = lax.rem(row, NZ)
    y = lax.rem(row // NZ, NY)
    x = row // (NZ * NY)
    zl, core = col // 2, lax.rem(col, 2)

    def device(px, py, pz, c=None):
        return ((px * NY + py) * NZ + pz, col if c is None else c)

    def hop(axis, sign):
        if axis == "x":
            return device(lax.rem(x + sign + NX, NX), y, zh)
        return device(x, lax.rem(y + sign + NY, NY), zh)

    partners = [hop(a, s) for a in ("x", "y") for s in (1, -1)] + [device(x, y, 1 - zh)]
    if with_adj:
        others = [lax.rem(col + j, NC) for j in range(1, NC)]
        partners += [(row, c) for c in others]
    barrier = pltpu.get_barrier_semaphore()
    for p in partners:
        pl.semaphore_signal(barrier, inc=1, device_id=p, device_id_type=MESH)
    pl.semaphore_wait(barrier, len(partners))

    def slab_of(rel, half, slab, sub):
        ix = slice(None) if slab[0] is None else lax.rem(x + slab[0] + NX, NX)
        iy = slice(None) if slab[1] is None else lax.rem(y + slab[1] + NY, NY)
        iz = zh if rel == 0 else 1 - zh
        isub = slice(None) if sub is None else sub
        return nodes.at[ix, iy, iz, half, isub]

    order = {}
    flying = {}
    pending = []

    def remote(src, dst, sems, k, dev):
        c = pltpu.make_async_remote_copy(
            src_ref=src, dst_ref=dst, send_sem=sems[0].at[k], recv_sem=sems[1].at[k],
            device_id=dev, device_id_type=MESH)
        c.start()
        return c

    mine = nodes.at[x, y, zh]
    own = pltpu.make_async_copy(shard, mine, local)
    own.start()
    flying["z"] = remote(shard, mine, (send, recv), 0, device(x, y, 1 - zh))
    counter = 1
    adj = {}

    def issue(sends):
        nonlocal counter
        for key, rel, half, slab, sub, axis, sign in sends:
            dst = slab_of(rel, half, slab, sub)
            src = dst
            if rel == 0 and slab == (0, 0):
                src = shard.at[half] if sub is None else shard.at[half, sub]
            flying[key] = remote(src, dst, (send, recv), counter, hop(axis, sign))
            counter += 1

    waited_own = False
    waited = set()
    adj_started = False
    for slot, rel, half, needs, sends in ring_program():
        for key in needs:
            if key not in waited:
                flying[key].wait_recv()
                waited.add(key)
        if not waited_own and any(s[3] != (0, 0) for s in sends):
            own.wait()
            waited_own = True
        issue(sends)
        if with_adj and not adj_started and slot == 0 and half == 1:
            adj_started = True
            adj_own = [pltpu.make_async_copy(tiles, tiles_all.at[col], adj_local.at[0]),
                       pltpu.make_async_copy(cols, cols_all.at[col], adj_local.at[1])]
            for c in adj_own:
                c.start()
            across = [remote(tiles, tiles_all.at[col], (adj_send, adj_recv), j - 1,
                             (row, lax.rem(zl + j, 4) * 2 + core)) for j in range(1, 4)]
            twin = [remote(tiles, tiles_all.at[col], (adj_send, adj_recv), 3,
                           (row, zl * 2 + 1 - core))]
            ids = [remote(cols, cols_all.at[col], (adj_send, adj_recv), 7 + j,
                          (row, others[j])) for j in range(NC - 1)]
    if with_adj:
        for j in range(1, 4):
            across[j - 1].wait_recv()
            origin = lax.rem(zl + 4 - j, 4) * 2 + core
            piece = tiles_all.at[origin]
            twin.append(remote(piece, piece, (adj_send, adj_recv), 3 + j,
                               (row, zl * 2 + 1 - core)))
        for c in twin + ids:
            c.wait_recv()
        for c in across + twin + ids:
            c.wait_send()
        for c in adj_own:
            c.wait()
    for key in flying:
        flying[key].wait_send()


def gather(shard, tiles=None, cols=None, collective_id=0):
    with_adj = tiles is not None
    steps = 1 + sum(len(p[4]) for p in ring_program())
    out_shape = [jax.ShapeDtypeStruct((NX, NY, NZ, 2, 2, BLK, 2 * BLK), jnp.bfloat16)]
    args = [shard.reshape(2, 2, BLK, 2 * BLK)]
    scratch = [pltpu.SemaphoreType.DMA((steps,)), pltpu.SemaphoreType.DMA((steps,)),
               pltpu.SemaphoreType.DMA]
    if with_adj:
        out_shape += [jax.ShapeDtypeStruct((NC,) + tiles.shape, tiles.dtype),
                      jax.ShapeDtypeStruct((NC,) + cols.shape, cols.dtype)]
        args += [tiles, cols]
        scratch += [pltpu.SemaphoreType.DMA((14,)), pltpu.SemaphoreType.DMA((14,)),
                    pltpu.SemaphoreType.DMA((2,))]
    return pl.pallas_call(
        functools.partial(gather_kernel, with_adj),
        out_shape=out_shape,
        in_specs=[pl.BlockSpec(memory_space=pltpu.VMEM)] * len(args),
        out_specs=[pl.BlockSpec(memory_space=pl.ANY)] * len(out_shape),
        scratch_shapes=scratch,
        compiler_params=pltpu.CompilerParams(collective_id=collective_id, has_side_effects=True),
    )(*args)


def hop_kernel(packed, cols, tiles, nodes, out_ref, *packed_ref):
    for i in range(4):
        acc = jnp.zeros((BLK, 2 * BLK), jnp.float32)
        for j in range(NC):
            picked = jnp.concatenate([nodes[cols[j, i, s]] for s in range(8)], axis=0)
            acc += jnp.dot(tiles[j, i], picked, preferred_element_type=jnp.float32)
        total = acc[:, :BLK] + acc[:, BLK:]
        out_ref[pl.ds(i * BLK, BLK), :] = total
        if packed:
            packed_ref[0][pl.ds(i * BLK, BLK), :] = split_parts(total)


def hop(nodes, tiles, cols, packed):
    out_shape = [jax.ShapeDtypeStruct((256, BLK), jnp.float32)]
    if packed:
        out_shape.append(jax.ShapeDtypeStruct((256, 2 * BLK), jnp.bfloat16))
    return pl.pallas_call(
        functools.partial(hop_kernel, packed),
        out_shape=out_shape,
        in_specs=[pl.BlockSpec(memory_space=pltpu.SMEM)] + [pl.BlockSpec(memory_space=pltpu.VMEM)] * 2,
        out_specs=[pl.BlockSpec(memory_space=pltpu.VMEM)] * len(out_shape),
    )(cols, tiles, nodes.reshape(256, BLK, 2 * BLK))


def local(features, adj_values, adj_cols, adj_count):
    slots = lax.axis_index("col") * 8 + jnp.arange(8, dtype=jnp.int32)
    live = slots[None, :, None] < adj_count[:, None, None]
    tiles = jnp.where(live, adj_values, jnp.zeros_like(adj_values))
    tiles = tiles.reshape(4, 8, BLK, BLK).transpose(0, 2, 1, 3).reshape(4, BLK, 8 * BLK)
    cols = jnp.pad(adj_cols, ((0, 4), (0, 120)))
    nodes, tiles_all, cols_all = gather(pack(features), tiles, cols, collective_id=0)
    hop_one, shard = hop(nodes, tiles_all, cols_all, True)
    (second,) = gather(shard, collective_id=1)
    (hop_two,) = hop(second, tiles_all, cols_all, False)
    return hop_one, hop_two


def solution(mesh):
    in_specs = (P("row", "col"), P("row", "col", None), P("row", "col"), P("row"))
    out_specs = (P("row", "col"), P("row", "col"))
    return jax.shard_map(local, mesh=mesh, in_specs=in_specs, out_specs=out_specs, check_vma=False)
```

```python
import functools

import jax
import jax.numpy as jnp
from jax import lax
from jax.experimental import pallas as pl
from jax.experimental.pallas import tpu as pltpu
from jax.sharding import PartitionSpec as P

BLK = 64
NX, NY, NZ = 4, 8, 2
NC = 8
MESH = pl.DeviceIdType.MESH


def split_parts(x):
    hi = x.astype(jnp.bfloat16).astype(jnp.float32)
    return hi, x - hi


TOP = float(8191 << 6)


def encode(x):
    top = jnp.max(jnp.abs(x), axis=(0, 1), keepdims=True)
    u = jnp.minimum(jnp.abs(x) * jnp.where(top > 0, TOP / top, 0.0), TOP)
    shift = jnp.zeros(x.shape, jnp.int32)
    down = jnp.ones(x.shape, jnp.float32)
    for j in range(1, 7):
        above = u >= float(4096 << j)
        shift = jnp.where(above, j, shift)
        down = jnp.where(above, 0.5 ** j, down)
    code = shift * 4096 + jnp.floor(u * down + 0.5).astype(jnp.int32)
    code = jnp.where(x < 0, -code, code)
    low = jnp.concatenate([code[0:BLK], code[2 * BLK:3 * BLK]], axis=1)
    high = jnp.concatenate([code[BLK:2 * BLK], code[3 * BLK:]], axis=1)
    return high * 65536 + low, top * (1.0 / TOP)


def decode(code, scale):
    size = jnp.abs(code)
    shift = jnp.maximum((size >> 12) - 1, 0)
    value = (size - (shift << 12)) << shift
    return jnp.where(code < 0, -value, value).astype(jnp.float32) * scale


def pack_kernel(count, x_ref, cols_ref, tiles_ref, out_ref, scale_ref, cols_out, tiles_out):
    words, scale = encode(x_ref[...].T)
    out_ref[...] = words
    scale_ref[...] = jnp.broadcast_to(scale, (1, 2 * BLK))
    cols_out[...] = jnp.zeros((8, 128), jnp.int32)
    cols_out[0:4, 0:8] = cols_ref[...]
    slots = lax.axis_index("col") * 8 + lax.broadcasted_iota(jnp.int32, (8, 4096), 0)
    for i in range(4):
        tile = tiles_ref[i].astype(jnp.float32)
        tiles_out[i] = jnp.where(slots < count[i], tile, 0.0).astype(jnp.bfloat16)


def pack(features, adj_values, adj_cols, adj_count):
    vmem = pl.BlockSpec(memory_space=pltpu.VMEM)
    return pl.pallas_call(
        pack_kernel,
        out_shape=[jax.ShapeDtypeStruct((BLK, 2 * BLK), jnp.int32),
                   jax.ShapeDtypeStruct((1, 2 * BLK), jnp.float32),
                   jax.ShapeDtypeStruct((8, 128), jnp.int32),
                   jax.ShapeDtypeStruct((4, 8, 4096), jnp.bfloat16)],
        in_specs=[pl.BlockSpec(memory_space=pltpu.SMEM)] + [vmem] * 3,
        out_specs=[vmem] * 4,
    )(adj_count, features.T, adj_cols, adj_values)


def ring_program():
    def stream(rel, half):
        tag = (rel, half)
        first, second = ("x", "y") if half == 0 else ("y", "x")
        size = {"x": NX, "y": NY}

        def phase(axis, whole):
            n = size[axis]
            steps = []
            for t in range(1, n // 2 + 1):
                sends = []
                for sign in (1, -1):
                    off = -sign * (t - 1)
                    slab = (off, whole) if axis == "x" else (whole, off)
                    sub = None if t < n // 2 else (0 if sign == 1 else 1)
                    sends.append(((tag, axis, t, sign), rel, half, slab, sub, axis, sign))
                steps.append(sends)
            return steps

        return phase(first, 0) + phase(second, None)

    program = []
    for rel in (0, 1):
        for half in (0, 1):
            steps = stream(rel, half)
            for t, sends in enumerate(steps):
                needs = [] if t == 0 else [s[0] for s in steps[t - 1]]
                if t == 0 and rel == 1:
                    needs = ["z"]
                program.append((t + 2 * rel, rel, half, needs, sends))
            program.append((len(steps) + 2 * rel, rel, half, [s[0] for s in steps[-1]], []))
    program.sort(key=lambda p: p[0])
    return program


def gather_kernel(with_adj, *refs):
    if with_adj:
        (shard, scale, tiles, cols, nodes, scales, tiles_all, cols_all,
         send, recv, scale_send, scale_recv, local, adj_send, adj_recv, adj_local) = refs
    else:
        shard, scale, nodes, scales, send, recv, scale_send, scale_recv, local = refs
    row = lax.axis_index("row")
    col = lax.axis_index("col")
    zh = lax.rem(row, NZ)
    y = lax.rem(row // NZ, NY)
    x = row // (NZ * NY)
    zl, core = col // 2, lax.rem(col, 2)

    def device(px, py, pz, c=None):
        return ((px * NY + py) * NZ + pz, col if c is None else c)

    def hop(axis, sign):
        if axis == "x":
            return device(lax.rem(x + sign + NX, NX), y, zh)
        return device(x, lax.rem(y + sign + NY, NY), zh)

    partners = [hop(a, s) for a in ("x", "y") for s in (1, -1)] + [device(x, y, 1 - zh)]
    if with_adj:
        others = [lax.rem(col + j, NC) for j in range(1, NC)]
        partners += [(row, c) for c in others]
    barrier = pltpu.get_barrier_semaphore()
    for p in partners:
        pl.semaphore_signal(barrier, inc=1, device_id=p, device_id_type=MESH)
    pl.semaphore_wait(barrier, len(partners))

    def slab_of(rel, half, slab, sub):
        ix = slice(None) if slab[0] is None else lax.rem(x + slab[0] + NX, NX)
        iy = slice(None) if slab[1] is None else lax.rem(y + slab[1] + NY, NY)
        iz = zh if rel == 0 else 1 - zh
        isub = slice(None) if sub is None else sub
        return nodes.at[ix, iy, iz, half, isub], scales.at[ix, iy, iz]

    flying = {}
    riding = {}

    def remote(src, dst, sems, k, dev):
        c = pltpu.make_async_remote_copy(
            src_ref=src, dst_ref=dst, send_sem=sems[0].at[k], recv_sem=sems[1].at[k],
            device_id=dev, device_id_type=MESH)
        c.start()
        return c

    mine = nodes.at[x, y, zh]
    mine_scale = scales.at[x, y, zh]
    own = [pltpu.make_async_copy(shard, mine, local.at[0]),
           pltpu.make_async_copy(scale, mine_scale, local.at[1])]
    for c in own:
        c.start()
    flying["z"] = remote(shard, mine, (send, recv), 0, device(x, y, 1 - zh))
    riding["z"] = remote(scale, mine_scale, (scale_send, scale_recv), 0, device(x, y, 1 - zh))
    counter = 1
    adj = {}

    def issue(sends):
        nonlocal counter
        for key, rel, half, slab, sub, axis, sign in sends:
            dst, dst_scale = slab_of(rel, half, slab, sub)
            src, src_scale = dst, dst_scale
            if rel == 0 and slab == (0, 0):
                src, src_scale = shard.at[half], scale
            flying[key] = remote(src, dst, (send, recv), counter, hop(axis, sign))
            if half == 0 and sub in (None, 0):
                riding[key] = remote(src_scale, dst_scale, (scale_send, scale_recv),
                                     len(riding), hop(axis, sign))
            counter += 1

    waited_own = False
    waited = set()
    adj_started = False
    for slot, rel, half, needs, sends in ring_program():
        for key in needs:
            if key not in waited:
                flying[key].wait_recv()
                if key in riding:
                    riding[key].wait_recv()
                waited.add(key)
        if not waited_own and any(s[3] != (0, 0) for s in sends):
            for c in own:
                c.wait()
            waited_own = True
        issue(sends)
        if with_adj and not adj_started and slot == 0 and half == 1:
            adj_started = True
            adj_own = [pltpu.make_async_copy(tiles, tiles_all.at[col], adj_local.at[0]),
                       pltpu.make_async_copy(cols, cols_all.at[col], adj_local.at[1])]
            for c in adj_own:
                c.start()
            across = [remote(tiles, tiles_all.at[col], (adj_send, adj_recv), j - 1,
                             (row, lax.rem(zl + j, 4) * 2 + core)) for j in range(1, 4)]
            twin = [remote(tiles, tiles_all.at[col], (adj_send, adj_recv), 3,
                           (row, zl * 2 + 1 - core))]
            ids = [remote(cols, cols_all.at[col], (adj_send, adj_recv), 7 + j,
                          (row, others[j])) for j in range(NC - 1)]
    if with_adj:
        for j in range(1, 4):
            across[j - 1].wait_recv()
            origin = lax.rem(zl + 4 - j, 4) * 2 + core
            piece = tiles_all.at[origin]
            twin.append(remote(piece, piece, (adj_send, adj_recv), 3 + j,
                               (row, zl * 2 + 1 - core)))
        for c in twin + ids:
            c.wait_recv()
        for c in across + twin + ids:
            c.wait_send()
        for c in adj_own:
            c.wait()
    for copy in list(flying.values()) + list(riding.values()):
        copy.wait_send()


def gather(shard, scale, tiles=None, cols=None, collective_id=0):
    with_adj = tiles is not None
    steps = 1 + sum(len(p[4]) for p in ring_program())
    rides = 1 + sum(half == 0 and sub in (None, 0)
                    for p in ring_program() for _, _, half, _, sub, _, _ in p[4])
    out_shape = [jax.ShapeDtypeStruct((NX, NY, NZ, 2, 2, 16, 128), jnp.int32),
                 jax.ShapeDtypeStruct((NX, NY, NZ, 1, 128), jnp.float32)]
    args = [shard.reshape(2, 2, 16, 128), scale]
    scratch = [pltpu.SemaphoreType.DMA((steps,)), pltpu.SemaphoreType.DMA((steps,)),
               pltpu.SemaphoreType.DMA((rides,)), pltpu.SemaphoreType.DMA((rides,)),
               pltpu.SemaphoreType.DMA((2,))]
    if with_adj:
        out_shape += [jax.ShapeDtypeStruct((NC,) + tiles.shape, tiles.dtype),
                      jax.ShapeDtypeStruct((NC,) + cols.shape, cols.dtype)]
        args += [tiles, cols]
        scratch += [pltpu.SemaphoreType.DMA((14,)), pltpu.SemaphoreType.DMA((14,)),
                    pltpu.SemaphoreType.DMA((2,))]
    return pl.pallas_call(
        functools.partial(gather_kernel, with_adj),
        out_shape=out_shape,
        in_specs=[pl.BlockSpec(memory_space=pltpu.VMEM)] * len(args),
        out_specs=[pl.BlockSpec(memory_space=pl.ANY)] * len(out_shape),
        scratch_shapes=scratch,
        compiler_params=pltpu.CompilerParams(collective_id=collective_id, has_side_effects=True),
    )(*args)


def hop_kernel(packed, cols, scales, tiles, words, out_ref, *rest):
    nodes = rest[-1]

    def unpack(r, _):
        scale = scales[r, 0, 0]
        word = words[r]
        high = (word + 32768) >> 16
        left = lax.broadcasted_iota(jnp.int32, (BLK, 2 * BLK), 1) < BLK
        for half, code in ((0, word - (high << 16)), (1, high)):
            hi, lo = split_parts(decode(code, scale))
            first = jnp.where(left, hi, pltpu.roll(lo, BLK, 1))
            second = jnp.where(left, pltpu.roll(hi, BLK, 1), lo)
            nodes[r * 4 + half] = first.astype(jnp.bfloat16)
            nodes[r * 4 + half + 2] = second.astype(jnp.bfloat16)
        return 0

    lax.fori_loop(0, NX * NY * NZ, unpack, 0, unroll=2)
    totals = []
    for i in range(4):
        acc = jnp.zeros((BLK, 2 * BLK), jnp.float32)
        for j in range(NC):
            picked = jnp.concatenate([nodes[cols[j, i, s]] for s in range(8)], axis=0)
            acc += jnp.dot(tiles[j, i], picked, preferred_element_type=jnp.float32)
        totals.append(acc[:, :BLK] + acc[:, BLK:])
    total = jnp.concatenate(totals, axis=0)
    out_ref[...] = total.T
    if packed:
        words_out, scale = encode(total)
        rest[0][...] = words_out
        rest[1][...] = jnp.broadcast_to(scale, (1, 2 * BLK))


def hop(words, scales, tiles, cols, packed):
    smem, vmem = (pl.BlockSpec(memory_space=m) for m in (pltpu.SMEM, pltpu.VMEM))
    out_shape = [jax.ShapeDtypeStruct((BLK, 256), jnp.float32)]
    if packed:
        out_shape += [jax.ShapeDtypeStruct((BLK, 2 * BLK), jnp.int32),
                      jax.ShapeDtypeStruct((1, 2 * BLK), jnp.float32)]
    out = pl.pallas_call(
        functools.partial(hop_kernel, packed),
        out_shape=out_shape,
        in_specs=[smem, smem, vmem, vmem],
        out_specs=[vmem] * len(out_shape),
        scratch_shapes=[pltpu.VMEM((256, BLK, 2 * BLK), jnp.bfloat16)],
    )(cols, scales.reshape(64, 1, 128), tiles, words.reshape(64, BLK, 128))
    return [out[0].T] + list(out[1:])


def local(features, adj_values, adj_cols, adj_count):
    shard, scale, cols, tiles = pack(features, adj_values, adj_cols, adj_count)
    tiles = tiles.reshape(4, 8, BLK, BLK).transpose(0, 2, 1, 3).reshape(4, BLK, 8 * BLK)
    nodes, scales, tiles_all, cols_all = gather(shard, scale, tiles, cols, collective_id=0)
    hop_one, shard, scale = hop(nodes, scales, tiles_all, cols_all, True)
    nodes, scales = gather(shard, scale, collective_id=1)
    (hop_two,) = hop(nodes, scales, tiles_all, cols_all, False)
    return hop_one, hop_two


def solution(mesh):
    in_specs = (P("row", "col"), P("row", "col", None), P("row", "col"), P("row"))
    out_specs = (P("row", "col"), P("row", "col"))
    return jax.shard_map(local, mesh=mesh, in_specs=in_specs, out_specs=out_specs, check_vma=False)
```

```python
import functools

import jax
import jax.numpy as jnp
from jax import lax
from jax.experimental import pallas as pl
from jax.experimental.pallas import tpu as pltpu
from jax.sharding import PartitionSpec as P

BLK = 64
NX, NY, NZ = 4, 8, 2
NC = 8
MODES = (("direct", "ring"), ("double", "ring"))
MESH = pl.DeviceIdType.MESH


def split_parts(x):
    hi = x.astype(jnp.bfloat16).astype(jnp.float32)
    return hi, x - hi


TOP = float(8191 << 6)


def encode(x):
    top = jnp.max(jnp.abs(x), axis=(0, 1), keepdims=True)
    u = jnp.minimum(jnp.abs(x) * jnp.where(top > 0, TOP / top, 0.0), TOP)
    shift = jnp.zeros(x.shape, jnp.int32)
    down = jnp.ones(x.shape, jnp.float32)
    for j in range(1, 7):
        above = u >= float(4096 << j)
        shift = jnp.where(above, j, shift)
        down = jnp.where(above, 0.5 ** j, down)
    code = shift * 4096 + jnp.floor(u * down + 0.5).astype(jnp.int32)
    code = jnp.where(x < 0, -code, code)
    low = jnp.concatenate([code[0:BLK], code[2 * BLK:3 * BLK]], axis=1)
    high = jnp.concatenate([code[BLK:2 * BLK], code[3 * BLK:]], axis=1)
    return high * 65536 + low, top * (1.0 / TOP)


def decode(code, scale):
    size = jnp.abs(code)
    shift = jnp.maximum((size >> 12) - 1, 0)
    value = (size - (shift << 12)) << shift
    return jnp.where(code < 0, -value, value).astype(jnp.float32) * scale


def pack_kernel(count, x_ref, cols_ref, tiles_ref, out_ref, scale_ref, cols_out, tiles_out):
    words, scale = encode(x_ref[...].T)
    out_ref[...] = words
    scale_ref[...] = jnp.broadcast_to(scale, (1, 2 * BLK))
    cols_out[...] = jnp.zeros((8, 128), jnp.int32)
    cols_out[0:4, 0:8] = cols_ref[...]
    slots = lax.axis_index("col") * 8 + lax.broadcasted_iota(jnp.int32, (8, 4096), 0)
    for i in range(4):
        tile = tiles_ref[i].astype(jnp.float32)
        tiles_out[i] = jnp.where(slots < count[i], tile, 0.0).astype(jnp.bfloat16)


def pack(features, adj_values, adj_cols, adj_count):
    vmem = pl.BlockSpec(memory_space=pltpu.VMEM)
    return pl.pallas_call(
        pack_kernel,
        out_shape=[jax.ShapeDtypeStruct((BLK, 2 * BLK), jnp.int32),
                   jax.ShapeDtypeStruct((1, 2 * BLK), jnp.float32),
                   jax.ShapeDtypeStruct((8, 128), jnp.int32),
                   jax.ShapeDtypeStruct((4, 8, 4096), jnp.bfloat16)],
        in_specs=[pl.BlockSpec(memory_space=pltpu.SMEM)] + [vmem] * 3,
        out_specs=[vmem] * 4,
    )(adj_count, features.T, adj_cols, adj_values)


def ring_program(modes=MODES, lag=1):
    size = {"x": NX, "y": NY}

    def moves(n, mode):
        if mode == "direct":
            return [[(0, None, 1), (0, None, -1), (0, None, 2)]]
        if mode == "double":
            return [[(0, None, 1), (0, None, -1), (0, None, 2), (0, None, -2)],
                    [(-2, None, 1), (2, None, -1), (-2, 0, 2), (2, 1, -2)]]
        last = n // 2
        return [[(-sign * (t - 1), None if t < last else (0 if sign == 1 else 1), sign)
                 for sign in (1, -1)] for t in range(1, last + 1)]

    def stream(rel, half):
        steps = []
        for turn in (0, 1):
            axis = "xy"[turn ^ half]
            for t, step in enumerate(moves(size[axis], modes[half][turn])):
                sends = []
                for off, sub, jump in step:
                    whole = 0 if turn == 0 else None
                    slab = (off, whole) if axis == "x" else (whole, off)
                    sends.append(((rel, half, axis, t, jump), rel, half, slab, sub, axis, jump))
                steps.append(sends)
        return steps

    program = []
    for rel in (0, 1):
        for half in (0, 1):
            steps = stream(rel, half)
            for t, sends in enumerate(steps):
                needs = (["z"] if rel == 1 else []) if t == 0 else [s[0] for s in steps[t - 1]]
                program.append((t + lag * rel, rel, half, needs, sends))
            program.append((len(steps) + lag * rel, rel, half, [s[0] for s in steps[-1]], []))
    program.sort(key=lambda p: p[0])
    return program


def gather_kernel(with_adj, *refs):
    if with_adj:
        (shard, scale, tiles, cols, nodes, scales, tiles_all, cols_all,
         send, recv, scale_send, scale_recv, local, adj_send, adj_recv, adj_local) = refs
    else:
        shard, scale, nodes, scales, send, recv, scale_send, scale_recv, local = refs
    row = lax.axis_index("row")
    col = lax.axis_index("col")
    zh = lax.rem(row, NZ)
    y = lax.rem(row // NZ, NY)
    x = row // (NZ * NY)
    zl, core = col // 2, lax.rem(col, 2)

    def device(px, py, pz, c=None):
        return ((px * NY + py) * NZ + pz, col if c is None else c)

    def hop(axis, sign):
        if axis == "x":
            return device(lax.rem(x + sign + NX, NX), y, zh)
        return device(x, lax.rem(y + sign + NY, NY), zh)

    partners = [hop("x", s) for s in (1, -1, 2)] + [hop("y", s) for s in (1, -1, 2, -2)] + [device(x, y, 1 - zh)]
    if with_adj:
        others = [lax.rem(col + j, NC) for j in range(1, NC)]
        partners += [(row, c) for c in others]
    barrier = pltpu.get_barrier_semaphore()
    for p in partners:
        pl.semaphore_signal(barrier, inc=1, device_id=p, device_id_type=MESH)
    pl.semaphore_wait(barrier, len(partners))

    def slab_of(rel, half, slab, sub):
        ix = slice(None) if slab[0] is None else lax.rem(x + slab[0] + NX, NX)
        iy = slice(None) if slab[1] is None else lax.rem(y + slab[1] + NY, NY)
        iz = zh if rel == 0 else 1 - zh
        isub = slice(None) if sub is None else sub
        return nodes.at[ix, iy, iz, half, isub], scales.at[ix, iy, iz]

    flying = {}
    riding = {}

    def remote(src, dst, sems, k, dev):
        c = pltpu.make_async_remote_copy(
            src_ref=src, dst_ref=dst, send_sem=sems[0].at[k], recv_sem=sems[1].at[k],
            device_id=dev, device_id_type=MESH)
        c.start()
        return c

    mine = nodes.at[x, y, zh]
    mine_scale = scales.at[x, y, zh]
    own = [pltpu.make_async_copy(shard, mine, local.at[0]),
           pltpu.make_async_copy(scale, mine_scale, local.at[1])]
    for c in own:
        c.start()
    flying["z"] = remote(shard, mine, (send, recv), 0, device(x, y, 1 - zh))
    riding["z"] = remote(scale, mine_scale, (scale_send, scale_recv), 0, device(x, y, 1 - zh))
    counter = 1
    adj = {}

    def issue(sends):
        nonlocal counter
        for key, rel, half, slab, sub, axis, sign in sends:
            dst, dst_scale = slab_of(rel, half, slab, sub)
            src, src_scale = dst, dst_scale
            if rel == 0 and slab == (0, 0):
                src, src_scale = shard.at[half], scale
            flying[key] = remote(src, dst, (send, recv), counter, hop(axis, sign))
            if half == 0 and sub in (None, 0):
                riding[key] = remote(src_scale, dst_scale, (scale_send, scale_recv),
                                     len(riding), hop(axis, sign))
            counter += 1

    waited_own = False
    waited = set()
    adj_started = False
    for slot, rel, half, needs, sends in ring_program():
        for key in needs:
            if key not in waited:
                flying[key].wait_recv()
                if key in riding:
                    riding[key].wait_recv()
                waited.add(key)
        if not waited_own and any(s[3] != (0, 0) for s in sends):
            for c in own:
                c.wait()
            waited_own = True
        issue(sends)
        if with_adj and not adj_started and slot == 0 and half == 1:
            adj_started = True
            adj_own = [pltpu.make_async_copy(tiles, tiles_all.at[col], adj_local.at[0]),
                       pltpu.make_async_copy(cols, cols_all.at[col], adj_local.at[1])]
            for c in adj_own:
                c.start()
            across = [remote(tiles, tiles_all.at[col], (adj_send, adj_recv), j - 1,
                             (row, lax.rem(zl + j, 4) * 2 + core)) for j in range(1, 4)]
            twin = [remote(tiles, tiles_all.at[col], (adj_send, adj_recv), 3,
                           (row, zl * 2 + 1 - core))]
            ids = [remote(cols, cols_all.at[col], (adj_send, adj_recv), 7 + j,
                          (row, others[j])) for j in range(NC - 1)]
    if with_adj:
        for j in range(1, 4):
            across[j - 1].wait_recv()
            origin = lax.rem(zl + 4 - j, 4) * 2 + core
            piece = tiles_all.at[origin]
            twin.append(remote(piece, piece, (adj_send, adj_recv), 3 + j,
                               (row, zl * 2 + 1 - core)))
        for c in twin + ids:
            c.wait_recv()
        for c in across + twin + ids:
            c.wait_send()
        for c in adj_own:
            c.wait()
    for copy in list(flying.values()) + list(riding.values()):
        copy.wait_send()


def gather(shard, scale, tiles=None, cols=None, collective_id=0):
    with_adj = tiles is not None
    steps = 1 + sum(len(p[4]) for p in ring_program())
    rides = 1 + sum(half == 0 and sub in (None, 0)
                    for p in ring_program() for _, _, half, _, sub, _, _ in p[4])
    out_shape = [jax.ShapeDtypeStruct((NX, NY, NZ, 2, 2, 16, 128), jnp.int32),
                 jax.ShapeDtypeStruct((NX, NY, NZ, 1, 128), jnp.float32)]
    args = [shard.reshape(2, 2, 16, 128), scale]
    scratch = [pltpu.SemaphoreType.DMA((steps,)), pltpu.SemaphoreType.DMA((steps,)),
               pltpu.SemaphoreType.DMA((rides,)), pltpu.SemaphoreType.DMA((rides,)),
               pltpu.SemaphoreType.DMA((2,))]
    if with_adj:
        out_shape += [jax.ShapeDtypeStruct((NC,) + tiles.shape, tiles.dtype),
                      jax.ShapeDtypeStruct((NC,) + cols.shape, cols.dtype)]
        args += [tiles, cols]
        scratch += [pltpu.SemaphoreType.DMA((14,)), pltpu.SemaphoreType.DMA((14,)),
                    pltpu.SemaphoreType.DMA((2,))]
    return pl.pallas_call(
        functools.partial(gather_kernel, with_adj),
        out_shape=out_shape,
        in_specs=[pl.BlockSpec(memory_space=pltpu.VMEM)] * len(args),
        out_specs=[pl.BlockSpec(memory_space=pltpu.VMEM)] * len(out_shape),
        scratch_shapes=scratch,
        compiler_params=pltpu.CompilerParams(collective_id=collective_id, has_side_effects=True),
    )(*args)


def hop_kernel(packed, cols, scales, tiles, words, out_ref, *rest):
    nodes = rest[-1]

    def unpack(r, _):
        scale = scales[r, 0, 0]
        word = words[r]
        high = (word + 32768) >> 16
        left = lax.broadcasted_iota(jnp.int32, (BLK, 2 * BLK), 1) < BLK
        for half, code in ((0, word - (high << 16)), (1, high)):
            hi, lo = split_parts(decode(code, scale))
            first = jnp.where(left, hi, pltpu.roll(lo, BLK, 1))
            second = jnp.where(left, pltpu.roll(hi, BLK, 1), lo)
            nodes[r * 4 + half] = first.astype(jnp.bfloat16)
            nodes[r * 4 + half + 2] = second.astype(jnp.bfloat16)
        return 0

    lax.fori_loop(0, NX * NY * NZ, unpack, 0, unroll=2)
    totals = []
    for i in range(4):
        acc = jnp.zeros((BLK, 2 * BLK), jnp.float32)
        for j in range(NC):
            picked = jnp.concatenate([nodes[cols[j, i, s]] for s in range(8)], axis=0)
            acc += jnp.dot(tiles[j, i], picked, preferred_element_type=jnp.float32)
        totals.append(acc[:, :BLK] + acc[:, BLK:])
    total = jnp.concatenate(totals, axis=0)
    out_ref[...] = total.T
    if packed:
        words_out, scale = encode(total)
        rest[0][...] = words_out
        rest[1][...] = jnp.broadcast_to(scale, (1, 2 * BLK))


def hop(words, scales, tiles, cols, packed):
    smem, vmem = (pl.BlockSpec(memory_space=m) for m in (pltpu.SMEM, pltpu.VMEM))
    out_shape = [jax.ShapeDtypeStruct((BLK, 256), jnp.float32)]
    if packed:
        out_shape += [jax.ShapeDtypeStruct((BLK, 2 * BLK), jnp.int32),
                      jax.ShapeDtypeStruct((1, 2 * BLK), jnp.float32)]
    out = pl.pallas_call(
        functools.partial(hop_kernel, packed),
        out_shape=out_shape,
        in_specs=[smem, smem, vmem, vmem],
        out_specs=[vmem] * len(out_shape),
        scratch_shapes=[pltpu.VMEM((256, BLK, 2 * BLK), jnp.bfloat16)],
    )(cols, scales.reshape(64, 1, 128), tiles, words.reshape(64, BLK, 128))
    return [out[0].T] + list(out[1:])


def local(features, adj_values, adj_cols, adj_count):
    shard, scale, cols, tiles = pack(features, adj_values, adj_cols, adj_count)
    tiles = tiles.reshape(4, 8, BLK, BLK).transpose(0, 2, 1, 3).reshape(4, BLK, 8 * BLK)
    nodes, scales, tiles_all, cols_all = gather(shard, scale, tiles, cols, collective_id=0)
    hop_one, shard, scale = hop(nodes, scales, tiles_all, cols_all, True)
    nodes, scales = gather(shard, scale, collective_id=1)
    (hop_two,) = hop(nodes, scales, tiles_all, cols_all, False)
    return hop_one, hop_two


def solution(mesh):
    in_specs = (P("row", "col"), P("row", "col", None), P("row", "col"), P("row"))
    out_specs = (P("row", "col"), P("row", "col"))
    return jax.shard_map(local, mesh=mesh, in_specs=in_specs, out_specs=out_specs, check_vma=False)
```

```python
import jax
import jax.numpy as jnp
from jax import lax
from jax.experimental import pallas as pl
from jax.experimental.pallas import tpu as pltpu
from jax.sharding import PartitionSpec as P

BLK = 64
NX, NY, NZ = 4, 8, 2
NC = 8
MODES = (("direct", "ring"), ("double", "ring"))
MESH = pl.DeviceIdType.MESH


def split_parts(x):
    hi = x.astype(jnp.bfloat16).astype(jnp.float32)
    return hi, x - hi


TOP = float(8191 << 6)


def encode(x):
    top = jnp.max(jnp.abs(x), axis=(0, 1), keepdims=True)
    u = jnp.minimum(jnp.abs(x) * jnp.where(top > 0, TOP / top, 0.0), TOP)
    shift = jnp.zeros(x.shape, jnp.int32)
    down = jnp.ones(x.shape, jnp.float32)
    for j in range(1, 7):
        above = u >= float(4096 << j)
        shift = jnp.where(above, j, shift)
        down = jnp.where(above, 0.5 ** j, down)
    code = shift * 4096 + jnp.floor(u * down + 0.5).astype(jnp.int32)
    code = jnp.where(x < 0, -code, code)
    low = jnp.concatenate([code[0:BLK], code[2 * BLK:3 * BLK]], axis=1)
    high = jnp.concatenate([code[BLK:2 * BLK], code[3 * BLK:]], axis=1)
    return high * 65536 + low, top * (1.0 / TOP)


def decode(code, scale):
    size = jnp.abs(code)
    shift = jnp.maximum((size >> 12) - 1, 0)
    value = (size - (shift << 12)) << shift
    return jnp.where(code < 0, -value, value).astype(jnp.float32) * scale


def pack_kernel(count, x_ref, cols_ref, tiles_ref, out_ref, scale_ref, cols_out, tiles_out):
    words, scale = encode(x_ref[...].T)
    out_ref[...] = words
    scale_ref[...] = jnp.broadcast_to(scale, (1, 2 * BLK))
    cols_out[...] = jnp.zeros((8, 128), jnp.int32)
    cols_out[0:4, 0:8] = cols_ref[...]
    slots = lax.axis_index("col") * 8 + lax.broadcasted_iota(jnp.int32, (8, 4096), 0)
    for i in range(4):
        tile = tiles_ref[i].astype(jnp.float32)
        tiles_out[i] = jnp.where(slots < count[i], tile, 0.0).astype(jnp.bfloat16)


def pack(features, adj_values, adj_cols, adj_count):
    vmem = pl.BlockSpec(memory_space=pltpu.VMEM)
    return pl.pallas_call(
        pack_kernel,
        out_shape=[jax.ShapeDtypeStruct((BLK, 2 * BLK), jnp.int32),
                   jax.ShapeDtypeStruct((1, 2 * BLK), jnp.float32),
                   jax.ShapeDtypeStruct((8, 128), jnp.int32),
                   jax.ShapeDtypeStruct((4, 8, 4096), jnp.bfloat16)],
        in_specs=[pl.BlockSpec(memory_space=pltpu.SMEM)] + [vmem] * 3,
        out_specs=[vmem] * 4,
    )(adj_count, features.T, adj_cols, adj_values)


def ring_program(modes=MODES, lag=1):
    size = {"x": NX, "y": NY}

    def moves(n, mode):
        if mode == "direct":
            return [[(0, None, 1), (0, None, -1), (0, None, 2)]]
        if mode == "double":
            return [[(0, None, 1), (0, None, -1), (0, None, 2), (0, None, -2)],
                    [(-2, None, 1), (2, None, -1), (-2, 0, 2), (2, 1, -2)]]
        last = n // 2
        return [[(-sign * (t - 1), None if t < last else (0 if sign == 1 else 1), sign)
                 for sign in (1, -1)] for t in range(1, last + 1)]

    def stream(rel, half):
        steps = []
        for turn in (0, 1):
            axis = "xy"[turn ^ half]
            for t, step in enumerate(moves(size[axis], modes[half][turn])):
                sends = []
                for off, sub, jump in step:
                    whole = 0 if turn == 0 else None
                    slab = (off, whole) if axis == "x" else (whole, off)
                    sends.append(((rel, half, axis, t, jump), rel, half, slab, sub, axis, jump))
                steps.append(sends)
        return steps

    program = []
    for rel in (0, 1):
        for half in (0, 1):
            steps = stream(rel, half)
            for t, sends in enumerate(steps):
                needs = (["z"] if rel == 1 else []) if t == 0 else [s[0] for s in steps[t - 1]]
                program.append((t + lag * rel, rel, half, needs, sends))
            program.append((len(steps) + lag * rel, rel, half, [s[0] for s in steps[-1]], []))
    program.sort(key=lambda p: p[0])
    return program


def unpack(words, scales, nodes, zh):
    left = lax.broadcasted_iota(jnp.int32, (BLK, 2 * BLK), 1) < BLK

    def one(q, _):
        x, y = q // NY, lax.rem(q, NY)
        r = q * NZ + zh
        scale = scales[x, y, zh]
        word = words[x, y, zh].reshape(BLK, 2 * BLK)
        high = (word + 32768) >> 16
        for half, code in ((0, word - (high << 16)), (1, high)):
            hi, lo = split_parts(decode(code, scale))
            first = jnp.where(left, hi, pltpu.roll(lo, BLK, 1))
            second = jnp.where(left, pltpu.roll(hi, BLK, 1), lo)
            nodes[r * 4 + half] = first.astype(jnp.bfloat16)
            nodes[r * 4 + half + 2] = second.astype(jnp.bfloat16)
        return 0

    lax.fori_loop(0, NX * NY, one, 0, unroll=2)


def multiply(cols, tiles, nodes):
    totals = []
    for i in range(4):
        acc = jnp.zeros((BLK, 2 * BLK), jnp.float32)
        for j in range(NC):
            picked = jnp.concatenate([nodes[cols[j, i, s]] for s in range(8)], axis=0)
            acc += jnp.dot(tiles[j, i], picked, preferred_element_type=jnp.float32)
        totals.append(acc[:, :BLK] + acc[:, BLK:])
    return jnp.concatenate(totals, axis=0)


def kernel(shard, scale, tiles, cols, out_one, out_two, words_one, words_two, scales_one,
           scales_two, tiles_all, cols_all, cols_smem, nodes, shard_two, scale_two, send, recv,
           scale_send, scale_recv, local, adj_send, adj_recv, adj_local):
    row = lax.axis_index("row")
    col = lax.axis_index("col")
    zh = lax.rem(row, NZ)
    y = lax.rem(row // NZ, NY)
    x = row // (NZ * NY)
    zl, core = col // 2, lax.rem(col, 2)

    def device(px, py, pz):
        return ((px * NY + py) * NZ + pz, col)

    def hop(axis, jump):
        if axis == "x":
            return device(lax.rem(x + jump + NX, NX), y, zh)
        return device(x, lax.rem(y + jump + NY, NY), zh)

    others = [lax.rem(col + j, NC) for j in range(1, NC)]
    partners = [hop("x", j) for j in (1, -1, 2)] + [hop("y", j) for j in (1, -1, 2, -2)]
    partners += [device(x, y, 1 - zh)] + [(row, c) for c in others]
    barrier = pltpu.get_barrier_semaphore()
    for p in partners:
        pl.semaphore_signal(barrier, inc=1, device_id=p, device_id_type=MESH)
    pl.semaphore_wait(barrier, len(partners))

    def remote(src, dst, sems, k, dev):
        c = pltpu.make_async_remote_copy(
            src_ref=src, dst_ref=dst, send_sem=sems[0].at[k], recv_sem=sems[1].at[k],
            device_id=dev, device_id_type=MESH)
        c.start()
        return c

    def gather(g, shard, scale, words, scales, after_start):
        main = (send.at[g], recv.at[g])
        side = (scale_send.at[g], scale_recv.at[g])

        def slab_of(rel, half, slab, sub):
            ix = slice(None) if slab[0] is None else lax.rem(x + slab[0] + NX, NX)
            iy = slice(None) if slab[1] is None else lax.rem(y + slab[1] + NY, NY)
            iz = zh if rel == 0 else 1 - zh
            isub = slice(None) if sub is None else sub
            return words.at[ix, iy, iz, half, isub], scales.at[ix, iy, iz]

        mine, mine_scale = words.at[x, y, zh], scales.at[x, y, zh]
        twin = device(x, y, 1 - zh)
        flying = {"z": remote(shard, mine, main, 0, twin)}
        riding = {"z": remote(scale, mine_scale, side, 0, twin)}
        own = [pltpu.make_async_copy(shard, mine, local.at[g, 0]),
               pltpu.make_async_copy(scale, mine_scale, local.at[g, 1])]
        for c in own:
            c.start()
        waited, started, waited_own, decoded = set(), False, False, False
        program = ring_program()
        for slot, rel, half, needs, sends in program:
            if slot > 0 and not started:
                started = True
                after_start()
            if slot == program[-1][0] and not decoded:
                decoded = True
                unpack(words, scales, nodes, zh)
            for key in needs:
                if key not in waited:
                    flying[key].wait_recv()
                    if key in riding:
                        riding[key].wait_recv()
                    waited.add(key)
            if not waited_own and any(s[3] != (0, 0) for s in sends):
                for c in own:
                    c.wait()
                waited_own = True
            for key, rel, half, slab, sub, axis, jump in sends:
                dst, dst_scale = slab_of(rel, half, slab, sub)
                src, src_scale = dst, dst_scale
                if rel == 0 and slab == (0, 0):
                    src, src_scale = shard.at[half], scale
                flying[key] = remote(src, dst, main, len(flying), hop(axis, jump))
                if half == 0 and sub in (None, 0):
                    riding[key] = remote(src_scale, dst_scale, side, len(riding), hop(axis, jump))
        unpack(words, scales, nodes, 1 - zh)
        return list(flying.values()) + list(riding.values())

    adj = []

    def start_adj():
        sems = (adj_send, adj_recv)
        adj.extend([
            [remote(tiles, tiles_all.at[col], sems, j - 1,
                    (row, lax.rem(zl + j, 4) * 2 + core)) for j in range(1, 4)],
            [remote(tiles, tiles_all.at[col], sems, 3, (row, zl * 2 + 1 - core))],
            [remote(cols, cols_all.at[col], sems, 7 + j, (row, others[j]))
             for j in range(NC - 1)],
            [pltpu.make_async_copy(tiles, tiles_all.at[col], adj_local.at[0]),
             pltpu.make_async_copy(cols, cols_all.at[col], adj_local.at[1])]])
        for c in adj[3]:
            c.start()

    sent = gather(0, shard, scale, words_one, scales_one, start_adj)
    across, twin, ids, adj_own = adj
    for j in range(1, 4):
        across[j - 1].wait_recv()
        piece = tiles_all.at[lax.rem(zl + 4 - j, 4) * 2 + core]
        twin.append(remote(piece, piece, (adj_send, adj_recv), 3 + j, (row, zl * 2 + 1 - core)))
    for c in ids:
        c.wait_recv()
    for c in adj_own:
        c.wait()
    to_smem = pltpu.make_async_copy(cols_all, cols_smem, adj_local.at[2])
    to_smem.start()
    to_smem.wait()
    for c in twin:
        c.wait_recv()

    total = multiply(cols_smem, tiles_all, nodes)
    codes, top = encode(total)
    shard_two[...] = codes.reshape(2, 2, 16, 2 * BLK)
    scale_two[...] = jnp.broadcast_to(top, (1, 2 * BLK))
    out_one[...] = total.T
    sent += gather(1, shard_two, scale_two, words_two, scales_two, lambda: None)
    out_two[...] = multiply(cols_smem, tiles_all, nodes).T
    for c in sent + across + twin + ids:
        c.wait_send()


def two_hops(shard, scale, tiles, cols):
    program = ring_program()
    sends = [s for p in program for s in p[4]]
    steps = 1 + len(sends)
    rides = 1 + sum(s[2] == 0 and s[4] in (None, 0) for s in sends)
    vmem = pl.BlockSpec(memory_space=pltpu.VMEM)
    dma = pltpu.SemaphoreType.DMA
    words = pltpu.VMEM((NX, NY, NZ, 2, 2, 16, 128), jnp.int32)
    scales = pltpu.VMEM((NX, NY, NZ, 1, 128), jnp.float32)
    one, two = pl.pallas_call(
        kernel,
        out_shape=[jax.ShapeDtypeStruct((BLK, 256), jnp.float32)] * 2,
        in_specs=[vmem] * 4,
        out_specs=[vmem] * 2,
        scratch_shapes=[words, words, scales, scales,
                        pltpu.VMEM((NC,) + tiles.shape, tiles.dtype),
                        pltpu.VMEM((NC,) + cols.shape, cols.dtype),
                        pltpu.SMEM((NC,) + cols.shape, cols.dtype),
                        pltpu.VMEM((256, BLK, 2 * BLK), jnp.bfloat16),
                        pltpu.VMEM((2, 2, 16, 128), jnp.int32),
                        pltpu.VMEM((1, 128), jnp.float32),
                        dma((2, steps)), dma((2, steps)), dma((2, rides)), dma((2, rides)),
                        dma((2, 2)), dma((14,)), dma((14,)), dma((3,))],
        compiler_params=pltpu.CompilerParams(collective_id=0, has_side_effects=True),
    )(shard.reshape(2, 2, 16, 128), scale, tiles, cols)
    return one.T, two.T


def local(features, adj_values, adj_cols, adj_count):
    shard, scale, cols, tiles = pack(features, adj_values, adj_cols, adj_count)
    tiles = tiles.reshape(4, 8, BLK, BLK).transpose(0, 2, 1, 3).reshape(4, BLK, 8 * BLK)
    return two_hops(shard, scale, tiles, cols)


def solution(mesh):
    in_specs = (P("row", "col"), P("row", "col", None), P("row", "col"), P("row"))
    out_specs = (P("row", "col"), P("row", "col"))
    return jax.shard_map(local, mesh=mesh, in_specs=in_specs, out_specs=out_specs, check_vma=False)
```

```python
import jax
import jax.numpy as jnp
from jax import lax
from jax.experimental import pallas as pl
from jax.experimental.pallas import tpu as pltpu
from jax.sharding import PartitionSpec as P

BLK = 64
NX, NY, NZ = 4, 8, 2
NC = 8
MODES = (("direct", "ring"), ("double", "ring"))
MESH = pl.DeviceIdType.MESH


def split_parts(x):
    hi = x.astype(jnp.bfloat16).astype(jnp.float32)
    return hi, x - hi


TOP = float(8191 << 6)


def encode(x):
    top = jnp.max(jnp.abs(x), axis=(0, 1), keepdims=True)
    u = jnp.minimum(jnp.abs(x) * jnp.where(top > 0, TOP / top, 0.0), TOP)
    shift = jnp.zeros(x.shape, jnp.int32)
    down = jnp.ones(x.shape, jnp.float32)
    for j in range(1, 7):
        above = u >= float(4096 << j)
        shift = jnp.where(above, j, shift)
        down = jnp.where(above, 0.5 ** j, down)
    code = shift * 4096 + jnp.floor(u * down + 0.5).astype(jnp.int32)
    code = jnp.where(x < 0, -code, code)
    low = jnp.concatenate([code[0:BLK], code[2 * BLK:3 * BLK]], axis=1)
    high = jnp.concatenate([code[BLK:2 * BLK], code[3 * BLK:]], axis=1)
    return high * 65536 + low, top * (1.0 / TOP)


def decode(code, scale):
    size = jnp.abs(code)
    shift = jnp.maximum((size >> 12) - 1, 0)
    value = (size - (shift << 12)) << shift
    return jnp.where(code < 0, -value, value).astype(jnp.float32) * scale


def pack_kernel(count, x_ref, cols_ref, tiles_ref, out_ref, scale_ref, cols_out, tiles_out):
    words, scale = encode(x_ref[...].T)
    out_ref[...] = words
    scale_ref[...] = jnp.broadcast_to(scale, (1, 2 * BLK))
    cols_out[...] = jnp.zeros((8, 128), jnp.int32)
    cols_out[0:4, 0:8] = cols_ref[...]
    slots = lax.axis_index("col") * 8 + lax.broadcasted_iota(jnp.int32, (8, 4096), 0)
    for i in range(4):
        tile = tiles_ref[i].astype(jnp.float32)
        tiles_out[i] = jnp.where(slots < count[i], tile, 0.0).astype(jnp.bfloat16)


def pack(features, adj_values, adj_cols, adj_count):
    vmem = pl.BlockSpec(memory_space=pltpu.VMEM)
    return pl.pallas_call(
        pack_kernel,
        out_shape=[jax.ShapeDtypeStruct((BLK, 2 * BLK), jnp.int32),
                   jax.ShapeDtypeStruct((1, 2 * BLK), jnp.float32),
                   jax.ShapeDtypeStruct((8, 128), jnp.int32),
                   jax.ShapeDtypeStruct((4, 8, 4096), jnp.bfloat16)],
        in_specs=[pl.BlockSpec(memory_space=pltpu.SMEM)] + [vmem] * 3,
        out_specs=[vmem] * 4,
    )(adj_count, features.T, adj_cols, adj_values)


def ring_program(modes=MODES, lag=1):
    size = {"x": NX, "y": NY}

    def moves(n, mode):
        if mode == "direct":
            return [[(0, None, 1), (0, None, -1), (0, None, 2)]]
        if mode == "double":
            return [[(0, None, 1), (0, None, -1), (0, None, 2), (0, None, -2)],
                    [(-2, None, 1), (2, None, -1), (-2, 0, 2), (2, 1, -2)]]
        last = n // 2
        return [[(-sign * (t - 1), None if t < last else (0 if sign == 1 else 1), sign)
                 for sign in (1, -1)] for t in range(1, last + 1)]

    def stream(rel, half):
        steps = []
        for turn in (0, 1):
            axis = "xy"[turn ^ half]
            for t, step in enumerate(moves(size[axis], modes[half][turn])):
                sends = []
                for off, sub, jump in step:
                    whole = 0 if turn == 0 else None
                    slab = (off, whole) if axis == "x" else (whole, off)
                    sends.append(((rel, half, axis, t, jump), rel, half, slab, sub, axis, jump))
                steps.append(sends)
        return steps

    program = []
    for rel in (0, 1):
        for half in (0, 1):
            steps = stream(rel, half)
            for t, sends in enumerate(steps):
                needs = (["z"] if rel == 1 else []) if t == 0 else [s[0] for s in steps[t - 1]]
                program.append((t + lag * rel, rel, half, needs, sends))
            program.append((len(steps) + lag * rel, rel, half, [s[0] for s in steps[-1]], []))
    program.sort(key=lambda p: p[0])
    return program


def unpack(words, scales, nodes, zh):
    left = lax.broadcasted_iota(jnp.int32, (BLK, 2 * BLK), 1) < BLK

    def one(q, _):
        x, y = q // NY, lax.rem(q, NY)
        r = q * NZ + zh
        scale = scales[x, y, zh]
        word = words[x, y, zh].reshape(BLK, 2 * BLK)
        high = (word + 32768) >> 16
        for half, code in ((0, word - (high << 16)), (1, high)):
            hi, lo = split_parts(decode(code, scale))
            first = jnp.where(left, hi, pltpu.roll(lo, BLK, 1))
            second = jnp.where(left, pltpu.roll(hi, BLK, 1), lo)
            nodes[r * 4 + half] = first.astype(jnp.bfloat16)
            nodes[r * 4 + half + 2] = second.astype(jnp.bfloat16)
        return 0

    lax.fori_loop(0, NX * NY, one, 0, unroll=2)


def multiply(cols, tiles, nodes, parts, accs):
    out = []
    for i in range(4):
        acc = accs[i]
        for j in parts:
            picked = jnp.concatenate([nodes[cols[j, i, s]] for s in range(8)], axis=0)
            acc += jnp.dot(tiles[j, i], picked, preferred_element_type=jnp.float32)
        out.append(acc)
    return out


def join(accs):
    return jnp.concatenate([acc[:, :BLK] + acc[:, BLK:] for acc in accs], axis=0)


def kernel(shard, scale, tiles, cols, out_one, out_two, words_one, words_two, scales_one,
           scales_two, tiles_all, cols_all, cols_smem, nodes, shard_two, scale_two, send, recv,
           scale_send, scale_recv, local, adj_send, adj_recv, adj_local):
    row = lax.axis_index("row")
    col = lax.axis_index("col")
    zh = lax.rem(row, NZ)
    y = lax.rem(row // NZ, NY)
    x = row // (NZ * NY)
    zl, core = col // 2, lax.rem(col, 2)

    def device(px, py, pz):
        return ((px * NY + py) * NZ + pz, col)

    def hop(axis, jump):
        if axis == "x":
            return device(lax.rem(x + jump + NX, NX), y, zh)
        return device(x, lax.rem(y + jump + NY, NY), zh)

    others = [lax.rem(col + j, NC) for j in range(1, NC)]
    partners = [hop("x", j) for j in (1, -1, 2)] + [hop("y", j) for j in (1, -1, 2, -2)]
    partners += [device(x, y, 1 - zh)] + [(row, c) for c in others]
    barrier = pltpu.get_barrier_semaphore()
    for p in partners:
        pl.semaphore_signal(barrier, inc=1, device_id=p, device_id_type=MESH)
    pl.semaphore_wait(barrier, len(partners))

    def remote(src, dst, sems, k, dev):
        c = pltpu.make_async_remote_copy(
            src_ref=src, dst_ref=dst, send_sem=sems[0].at[k], recv_sem=sems[1].at[k],
            device_id=dev, device_id_type=MESH)
        c.start()
        return c

    def gather(g, shard, scale, words, scales, after_start):
        main = (send.at[g], recv.at[g])
        side = (scale_send.at[g], scale_recv.at[g])

        def slab_of(rel, half, slab, sub):
            ix = slice(None) if slab[0] is None else lax.rem(x + slab[0] + NX, NX)
            iy = slice(None) if slab[1] is None else lax.rem(y + slab[1] + NY, NY)
            iz = zh if rel == 0 else 1 - zh
            isub = slice(None) if sub is None else sub
            return words.at[ix, iy, iz, half, isub], scales.at[ix, iy, iz]

        mine, mine_scale = words.at[x, y, zh], scales.at[x, y, zh]
        twin = device(x, y, 1 - zh)
        flying = {"z": remote(shard, mine, main, 0, twin)}
        riding = {"z": remote(scale, mine_scale, side, 0, twin)}
        own = [pltpu.make_async_copy(shard, mine, local.at[g, 0]),
               pltpu.make_async_copy(scale, mine_scale, local.at[g, 1])]
        for c in own:
            c.start()
        waited, started, waited_own, decoded = set(), False, False, False
        program = ring_program()
        for slot, rel, half, needs, sends in program:
            if slot > 0 and not started:
                started = True
                after_start()
            if slot == program[-1][0] and not decoded:
                decoded = True
                unpack(words, scales, nodes, zh)
            for key in needs:
                if key not in waited:
                    flying[key].wait_recv()
                    if key in riding:
                        riding[key].wait_recv()
                    waited.add(key)
            if not waited_own and any(s[3] != (0, 0) for s in sends):
                for c in own:
                    c.wait()
                waited_own = True
            for key, rel, half, slab, sub, axis, jump in sends:
                dst, dst_scale = slab_of(rel, half, slab, sub)
                src, src_scale = dst, dst_scale
                if rel == 0 and slab == (0, 0):
                    src, src_scale = shard.at[half], scale
                flying[key] = remote(src, dst, main, len(flying), hop(axis, jump))
                if half == 0 and sub in (None, 0):
                    riding[key] = remote(src_scale, dst_scale, side, len(riding), hop(axis, jump))
        unpack(words, scales, nodes, 1 - zh)
        return list(flying.values()) + list(riding.values())

    adj = []

    def start_adj():
        sems = (adj_send, adj_recv)
        adj.extend([
            [remote(tiles, tiles_all.at[col], sems, j - 1,
                    (row, lax.rem(zl + j, 4) * 2 + core)) for j in range(1, 4)],
            [remote(tiles, tiles_all.at[col], sems, 3, (row, zl * 2 + 1 - core))],
            [remote(cols, cols_all.at[col], sems, 7 + j, (row, others[j]))
             for j in range(NC - 1)],
            [pltpu.make_async_copy(tiles, tiles_all.at[col], adj_local.at[0]),
             pltpu.make_async_copy(cols, cols_all.at[col], adj_local.at[1])]])
        for c in adj[3]:
            c.start()

    sent = gather(0, shard, scale, words_one, scales_one, start_adj)
    across, twin, ids, adj_own = adj
    for j in range(1, 4):
        across[j - 1].wait_recv()
        piece = tiles_all.at[lax.rem(zl + 4 - j, 4) * 2 + core]
        twin.append(remote(piece, piece, (adj_send, adj_recv), 3 + j, (row, zl * 2 + 1 - core)))
    for c in ids:
        c.wait_recv()
    for c in adj_own:
        c.wait()
    to_smem = pltpu.make_async_copy(cols_all, cols_smem, adj_local.at[2])
    to_smem.start()
    to_smem.wait()
    same = [z * 2 + core for z in range(NC // 2)]
    other = [z * 2 + 1 - core for z in range(NC // 2)]
    zero = [jnp.zeros((BLK, 2 * BLK), jnp.float32)] * 4
    accs = multiply(cols_smem, tiles_all, nodes, same, zero)
    for c in twin:
        c.wait_recv()
    total = join(multiply(cols_smem, tiles_all, nodes, other, accs))
    codes, top = encode(total)
    shard_two[...] = codes.reshape(2, 2, 16, 2 * BLK)
    scale_two[...] = jnp.broadcast_to(top, (1, 2 * BLK))
    out_one[...] = total.T
    sent += gather(1, shard_two, scale_two, words_two, scales_two, lambda: None)
    out_two[...] = join(multiply(cols_smem, tiles_all, nodes, same + other, zero)).T
    for c in sent + across + twin + ids:
        c.wait_send()


def two_hops(shard, scale, tiles, cols):
    program = ring_program()
    sends = [s for p in program for s in p[4]]
    steps = 1 + len(sends)
    rides = 1 + sum(s[2] == 0 and s[4] in (None, 0) for s in sends)
    vmem = pl.BlockSpec(memory_space=pltpu.VMEM)
    dma = pltpu.SemaphoreType.DMA
    words = pltpu.VMEM((NX, NY, NZ, 2, 2, 16, 128), jnp.int32)
    scales = pltpu.VMEM((NX, NY, NZ, 1, 128), jnp.float32)
    one, two = pl.pallas_call(
        kernel,
        out_shape=[jax.ShapeDtypeStruct((BLK, 256), jnp.float32)] * 2,
        in_specs=[vmem] * 4,
        out_specs=[vmem] * 2,
        scratch_shapes=[words, words, scales, scales,
                        pltpu.VMEM((NC,) + tiles.shape, tiles.dtype),
                        pltpu.VMEM((NC,) + cols.shape, cols.dtype),
                        pltpu.SMEM((NC,) + cols.shape, cols.dtype),
                        pltpu.VMEM((256, BLK, 2 * BLK), jnp.bfloat16),
                        pltpu.VMEM((2, 2, 16, 128), jnp.int32),
                        pltpu.VMEM((1, 128), jnp.float32),
                        dma((2, steps)), dma((2, steps)), dma((2, rides)), dma((2, rides)),
                        dma((2, 2)), dma((14,)), dma((14,)), dma((3,))],
        compiler_params=pltpu.CompilerParams(collective_id=0, has_side_effects=True),
    )(shard.reshape(2, 2, 16, 128), scale, tiles, cols)
    return one.T, two.T


def local(features, adj_values, adj_cols, adj_count):
    shard, scale, cols, tiles = pack(features, adj_values, adj_cols, adj_count)
    tiles = tiles.reshape(4, 8, BLK, BLK).transpose(0, 2, 1, 3).reshape(4, BLK, 8 * BLK)
    return two_hops(shard, scale, tiles, cols)


def solution(mesh):
    in_specs = (P("row", "col"), P("row", "col", None), P("row", "col"), P("row"))
    out_specs = (P("row", "col"), P("row", "col"))
    return jax.shard_map(local, mesh=mesh, in_specs=in_specs, out_specs=out_specs, check_vma=False)
```
